512 devices in a mesh: expert: 32 (over x, y), dp: 16 (over z, core).
Axes of the slice: x: 4, y: 8, z: 8, core: 2. Of those that a mesh axis runs over, the one named last changes fastest.
Arguments:
- tokens: bfloat16 [8192, 1664], P(('expert', 'dp')), may hold values from -6 to 6
- cotangent: bfloat16 [8192, 1664], P(('expert', 'dp')), may hold values from -1.1953125 to 1.1953125
- expert_ids: int32 [8192, 2], P(('expert', 'dp')), may hold values from 0 to 31, all different within a row; in each aligned block of 16 rows (0 to 15, 16 to 31, ...) at most 2 rows name the same one
- gates: bfloat16 [8192, 2], P(('expert', 'dp')), may hold values from 0.099609375 to 1
- w_in: bfloat16 [32, 1664, 4096], P('expert', None, 'dp'), may hold values from -0.15625 to 0.15625
- w_out: bfloat16 [32, 4096, 1664], P('expert', 'dp'), may hold values from -0.09375 to 0.09375
Outputs:
- token_grads: bfloat16 [8192, 1664], P(('expert', 'dp'))
- gate_grads: bfloat16 [8192, 2], P(('expert', 'dp'))
- grad_in_weights: bfloat16 [32, 1664, 4096], P('expert', None, 'dp')
- grad_out_weights: bfloat16 [32, 4096, 1664], P('expert', 'dp')
The draws below stay inside these ranges and needn't reach their ends.
Inputs may be any that keep to these rules, and one draw needn't show every extreme that they name: `expert_ids`: the two experts of a token differ, and no expert is named by more than 2 of the 16 tokens of one device.
All inputs are finite; a program needn't handle non-finite values.
Results may differ from the reference program's by a relative error of at most 0.019.
Values may be sent and summed in bfloat16 or wider, within the bound.
No kernel may reach another device: no remote copies, remote signals or barrier semaphores. Data moves between devices by JAX's collectives and lax.ppermute only.
A program may use at most 64 MiB of HBM per device.

```python
import math
import jax
import jax.numpy as jnp
import numpy as np
from jax import lax

D = 1664
FF = 4096
TOK_DEV = 16
EXPERTS = 32
CAP = 2
TOKENS = 8192
N_DP = 16


def shard_levels(stream_key, shape, shards, low, largest):
    gain, own = 1.0, jax.random.fold_in(stream_key, 6)
    for dim, shards_of in shards:
        draws = jnp.exp(jax.random.uniform(jax.random.fold_in(own, dim), (shards_of,), jnp.float32, low / len(shards), largest / len(shards)))
        gain = gain * jnp.repeat(draws, shape[dim] // shards_of).reshape([-1 if axis == dim else 1 for axis in range(len(shape))])
    return gain


def shared_out(stream_key, own, number, rows, amount, top, bound, lean):
    order = jax.random.permutation(stream_key, amount)
    packed, ordinary = portions_of(amount, rows * top, bound, lean, True), portions_of(amount, rows * top, bound, lean, False)
    places = jnp.arange(amount)

    def named(sizes, turn):
        used = int((sizes > 0).sum())
        fixed = max(1, used // 4)
        moved = fixed + (places - fixed + turn * (used - fixed)) % max(1, amount - fixed)
        return jnp.zeros((amount,), jnp.int32).at[order[jnp.where(places < fixed, places, moved)]].set(jnp.asarray(sizes, jnp.int32))

    sizes = jnp.where(number % 4 == 0, named(packed, number // 4), named(ordinary, number - number // 4 - 1))
    mixed = jax.random.permutation(jax.random.fold_in(own, 3), amount)
    donor, taker = mixed[0:amount // 2 * 2:2], mixed[1:amount // 2 * 2:2]
    slack = jnp.minimum(sizes[donor] - 1, bound - sizes[taker]) // 2
    slack = jnp.where((donor == order[0]) | (taker == order[0]) | (sizes[taker] == 0), 0, jnp.maximum(slack, 0))
    moved = jax.random.randint(jax.random.fold_in(own, 4), (amount // 2,), 0, 1 << 20) % (slack + 1)
    sizes = sizes.at[donor].add(-moved).at[taker].add(moved)
    members = jnp.searchsorted(jnp.cumsum(sizes), jnp.arange(rows * top), side="right").astype(jnp.int32)
    listing = members.reshape(top, rows).T
    listing = listing[jax.random.permutation(jax.random.fold_in(own, 1), rows)]
    turn = jax.random.randint(jax.random.fold_in(own, 2), (rows, 1), 0, top)
    return jnp.take_along_axis(listing, (jnp.arange(top)[None, :] + turn) % top, axis=1)


def portions_of(amount, total, most, skew, full):
    loads = [(1 << 20) // math.isqrt(grade ** skew) + 1 for grade in range(1, amount + 1)]
    largest = most if full else min(most, max(-(-total // amount), total * loads[0] // sum(loads)))
    least = 1 if total - largest >= amount - 1 else 0
    holding, spare = [largest] + [least] * (amount - 1), total - largest - least * (amount - 1)
    while spare > 0:
        free = [i for i in range(1, amount) if holding[i] < largest] or [i for i in range(1, amount) if holding[i] < most]
        mass, remaining = sum([loads[i] for i in free]), spare
        for i in free:
            extra = min(most - holding[i], max(1, remaining * loads[i] // mass), spare)
            holding[i] = holding[i] + extra
            spare = spare - extra
    return np.array(holding)


def normal_values(key, dims, width, reach, shards=(), kind=jnp.bfloat16):
    result = width * jax.random.normal(key, dims, jnp.float32)
    if shards:
        result = result * shard_levels(key, dims, shards, -0.22, 0.18)
    return jnp.clip(result, -reach, reach).astype(kind)


def setup_inputs(seed: int = 0) -> dict:
    seeds = jax.random.split(jax.random.key(seed), 7)
    tokens = normal_values(seeds[0], (TOKENS, D), 1.0, 6.0, ((0, 512),))
    cotangent = normal_values(seeds[1], (TOKENS, D), 0.2, 1.1953125, ((0, 512),))
    expert_ids_keys = jax.random.split(jax.random.fold_in(seeds[2], 1), TOKENS // TOK_DEV)
    expert_ids_turns = jax.random.permutation(jax.random.fold_in(seeds[2], 3), TOKENS // TOK_DEV)
    expert_ids = jax.vmap(lambda own, number: shared_out(jax.random.fold_in(seeds[2], 2), own, number, TOK_DEV, EXPERTS, 2, CAP, 2))(expert_ids_keys, expert_ids_turns).reshape((TOKENS, 2))
    gates = jnp.clip(0.099609375 + 0.9003906 * jax.random.uniform(seeds[3], (TOKENS, 2), jnp.float32) ** shard_levels(seeds[3], (TOKENS, 2), ((0, 512),), -0.2, 0.2), 0.099609375, 1.0).astype(jnp.bfloat16)
    w_in = normal_values(seeds[4], (EXPERTS, D, FF), D ** -0.5, 0.15625, ((0, 32), (2, 16)))
    w_out = normal_values(seeds[5], (EXPERTS, FF, D), FF ** -0.5, 0.09375, ((0, 32), (1, 16)))
    return {"tokens": tokens, "cotangent": cotangent, "expert_ids": expert_ids, "gates": gates, "w_in": w_in, "w_out": w_out}


def normal_parts(pre):
    cdf = 0.5 * (1.0 + lax.erf(pre * 0.7071067811865476))
    pdf = 0.3989422804014327 * jnp.exp(-0.5 * pre * pre)
    return cdf, pdf


def reference(tokens, cotangent, expert_ids, gates, w_in, w_out):
    blocks = TOKENS // TOK_DEV
    assign = 2 * TOK_DEV
    rows_per = blocks * CAP
    flat_ids = expert_ids.reshape(blocks, assign).astype(jnp.int32)
    onehot = (flat_ids[:, :, None] == jnp.arange(EXPERTS, dtype=jnp.int32)[None, None, :]).astype(jnp.int32)
    before = (jnp.cumsum(onehot, axis=1) - onehot).astype(jnp.int32)
    slot = jnp.sum(before * onehot, axis=2).astype(jnp.int32)
    block_num = jnp.arange(blocks, dtype=jnp.int32)[:, None]
    index = (flat_ids * rows_per + block_num * CAP + slot).reshape(-1).astype(jnp.int32)
    src_in = jnp.repeat(tokens, 2, axis=0)
    src_cot = jnp.repeat(cotangent, 2, axis=0)
    disp_in = jnp.zeros((EXPERTS * rows_per, D), jnp.bfloat16).at[index].set(src_in).reshape(EXPERTS, rows_per, D)
    disp_cot = jnp.zeros((EXPERTS * rows_per, D), jnp.bfloat16).at[index].set(src_cot).reshape(EXPERTS, rows_per, D)
    disp_gate = jnp.zeros((EXPERTS * rows_per,), jnp.bfloat16).at[index].set(gates.reshape(-1)).reshape(EXPERTS, rows_per)
    group = FF // N_DP

    def expert_step(items):
        x_rows, cot_rows, gate_rows, w_first, w_second = items
        pre = jnp.dot(x_rows, w_first, preferred_element_type=jnp.float32)
        cdf, pdf = normal_parts(pre)
        hidden = (pre * cdf).astype(jnp.bfloat16)
        back = lax.dot_general(cot_rows, w_second, (((1,), (1,)), ((), ())), preferred_element_type=jnp.float32)
        gate_f = gate_rows.astype(jnp.float32)[:, None]
        scaled = (gate_f * cot_rows.astype(jnp.float32)).astype(jnp.bfloat16)
        grad_second = lax.dot_general(hidden, scaled, (((0,), (0,)), ((), ())), preferred_element_type=jnp.float32).astype(jnp.bfloat16)
        pre_grad = (gate_f * back * (cdf + pre * pdf)).astype(jnp.bfloat16)
        grad_first = lax.dot_general(x_rows, pre_grad, (((0,), (0,)), ((), ())), preferred_element_type=jnp.float32).astype(jnp.bfloat16)
        parts = jnp.einsum("rjf,djf->jrd", pre_grad.astype(jnp.float32).reshape(rows_per, N_DP, group), w_first.astype(jnp.float32).reshape(D, N_DP, group))
        parts = lax.optimization_barrier(parts.astype(jnp.bfloat16)).astype(jnp.float32)
        row_grads = jnp.sum(parts, axis=0).astype(jnp.bfloat16)
        gate_out = jnp.sum(hidden.astype(jnp.float32) * back, axis=1).astype(jnp.bfloat16)
        return grad_first, grad_second, row_grads, gate_out

    grad_in_weights, grad_out_weights, row_grads, gate_out = lax.map(expert_step, (disp_in, disp_cot, disp_gate, w_in, w_out))
    flat_rows = row_grads.reshape(EXPERTS * rows_per, D)
    token_grads = jnp.sum(flat_rows[index].astype(jnp.float32).reshape(TOKENS, 2, D), axis=1).astype(jnp.bfloat16)
    gate_grads = gate_out.reshape(-1)[index].reshape(TOKENS, 2)
    return token_grads, gate_grads, grad_in_weights, grad_out_weights
```

```python
import functools

import jax
import jax.numpy as jnp
from jax import lax
from jax.experimental import pallas as pl
from jax.experimental.pallas import tpu as pltpu
from jax.sharding import PartitionSpec as P


LANES = 128
F32, BF16 = jnp.float32, jnp.bfloat16


def mm(a, b, dims):
    return lax.dot_general(a, b, (dims, ((), ())), preferred_element_type=F32)


def kernel_call(body, out_shapes, *args, flops=0):
    spec = pl.BlockSpec(memory_space=pltpu.VMEM)
    outs = tuple(jax.ShapeDtypeStruct(s, d) for s, d in out_shapes)
    moved = sum(a.size * a.dtype.itemsize for a in args)
    return pl.pallas_call(
        body,
        out_shape=outs,
        in_specs=[spec] * len(args),
        out_specs=tuple([spec] * len(outs)),
        cost_estimate=pl.CostEstimate(flops=flops, bytes_accessed=moved, transcendentals=0),
    )(*args)


def matches(ids, cap, rows):
    tok = ids.shape[1]
    row = lax.broadcasted_iota(jnp.int32, (rows, tok), 0)
    expert, slot = row // cap, row % cap
    hit0 = (ids[0:1, :] == expert).astype(F32)
    hit1 = (ids[1:2, :] == expert).astype(F32)
    hit = hit0 + hit1
    earlier = (
        lax.broadcasted_iota(jnp.int32, (tok, tok), 0)
        < lax.broadcasted_iota(jnp.int32, (tok, tok), 1)
    ).astype(F32)
    before = mm(hit, earlier, ((1,), (0,)))
    held = hit * (before == slot.astype(F32)).astype(F32)
    return held, hit0, hit1


def dispatch_body(cap, rows, tok_ref, cot_ref, ids_ref, gates_ref, send_ref):
    feat = tok_ref.shape[1]
    held, hit0, hit1 = matches(ids_ref[...], cap, rows)
    gates = gates_ref[...].astype(F32)
    gate = jnp.sum(held * (hit0 * gates[0:1, :] + hit1 * gates[1:2, :]), axis=1, keepdims=True)
    pick = held.astype(BF16)
    send_ref[:, :feat] = mm(pick, tok_ref[...], ((1,), (0,))).astype(BF16)
    send_ref[:, feat : 2 * feat] = mm(pick, cot_ref[...], ((1,), (0,))).astype(BF16)
    send_ref[:, 2 * feat :] = jnp.broadcast_to(gate, (rows, LANES)).astype(BF16)


def tail(gate_part):
    hi = gate_part.astype(BF16).astype(F32)
    lo = gate_part - hi
    lane = lax.broadcasted_iota(jnp.int32, (gate_part.shape[0], LANES), 1)
    return jnp.where(lane == 0, hi, jnp.where(lane == 1, lo, 0.0)).astype(BF16)


def work_body(a_ref, b_ref, w1_ref, w1p_ref, w2_ref, w2p_ref, hid_ref, pg_ref, part_ref):
    feat = w1_ref.shape[0]
    half = w1_ref.shape[1]
    n = a_ref.shape[0]
    x = jnp.concatenate([a_ref[:, :feat], b_ref[:, :feat]], axis=0)
    cot = jnp.concatenate([a_ref[:, feat : 2 * feat], b_ref[:, feat : 2 * feat]], axis=0)
    gate = jnp.concatenate([a_ref[:, 2 * feat :], b_ref[:, 2 * feat :]], axis=0).astype(F32)
    gate = gate[:, 0:1]
    gate_part = jnp.zeros((2 * n, 1), F32)
    part = jnp.zeros((2 * n, feat), F32)
    for at, v1, v2 in ((0, w1_ref, w2_ref), (half, w1p_ref, w2p_ref)):
        pre = mm(x, v1[...], ((1,), (0,)))
        back = mm(cot, v2[...], ((1,), (1,)))
        cdf = 0.5 * (1.0 + lax.erf(pre * 0.7071067811865476))
        pdf = 0.3989422804014327 * jnp.exp(-0.5 * pre * pre)
        hidden = (pre * cdf).astype(BF16)
        pre_grad = (gate * back * (cdf + pre * pdf)).astype(BF16)
        hid_ref[:, at : at + half] = hidden
        pg_ref[:, at : at + half] = pre_grad
        gate_part += jnp.sum(hidden.astype(F32) * back, axis=1, keepdims=True)
        part += mm(pre_grad, v1[...], ((1,), (1,)))
    part_ref[:, :feat] = part.astype(BF16)
    part_ref[:, feat:] = tail(gate_part)


def plus_body(feat, *refs):
    *ins, out_ref = refs
    out_ref[:, :feat] = sum(r[:, :feat].astype(F32) for r in ins).astype(BF16)
    g = sum(r[:, feat:].astype(F32) for r in ins)
    out_ref[:, feat:] = tail(g[:, 0:1] + g[:, 1:2])


def plus_head_body(feat, n, s_ref, part_ref, out_ref):
    out_ref[:, :feat] = (s_ref[:n, :feat].astype(F32) + part_ref[:n, :feat].astype(F32)).astype(BF16)
    g = s_ref[:n, feat:].astype(F32) + part_ref[:n, feat:].astype(F32)
    out_ref[:, feat:] = tail(g[:, 0:1] + g[:, 1:2])


def total_body(feat, n, sa_ref, sb_ref, part_ref, out_ref):
    out_ref[:, :feat] = (
        sa_ref[:, :feat].astype(F32) + sb_ref[:, :feat].astype(F32) + part_ref[n:, :feat].astype(F32)
    ).astype(BF16)
    g = sa_ref[:, feat:].astype(F32) + sb_ref[:, feat:].astype(F32) + part_ref[n:, feat:].astype(F32)
    out_ref[:, feat:] = tail(g[:, 0:1] + g[:, 1:2])


def combine_body(cap, rows, back_ref, ids_ref, tg_ref, gg_ref):
    feat = tg_ref.shape[1]
    held, hit0, hit1 = matches(ids_ref[...], cap, rows)
    tg_ref[...] = mm(held.astype(BF16), back_ref[:, :feat], ((0,), (0,))).astype(BF16)
    g = back_ref[:, feat:].astype(F32)
    g = g[:, 0:1] + g[:, 1:2]
    g0 = jnp.sum(held * hit0 * g, axis=0, keepdims=True)
    g1 = jnp.sum(held * hit1 * g, axis=0, keepdims=True)
    gg_ref[...] = jnp.concatenate([g0, g1], axis=0).astype(BF16)


def per_device(tokens, cotangent, expert_ids, gates, w_in, w_out):
    tok, feat = tokens.shape
    experts = lax.axis_size("expert")
    ndp = lax.axis_size("dp")
    nz = ndp // 2
    cap = max(2, 4 * tok // experts)
    rows = experts * cap
    hops = nz // 2
    wide = 2 * feat + LANES
    slim = feat + LANES

    swap = [(i, i ^ 1) for i in range(ndp)]

    def shifted(sign):
        pairs = []
        for z in range(nz):
            pairs.append((2 * z, 2 * ((z + sign) % nz)))
            pairs.append((2 * z + 1, 2 * ((z - sign) % nz) + 1))
        return pairs

    away, home = shifted(1), shifted(-1)

    def move(a, pairs):
        return lax.ppermute(a, "dp", pairs)

    w1 = w_in[0]
    w2 = w_out[0]
    half = w1.shape[1]
    w1p = move(w1, swap)
    w2p = move(w2, swap)

    ids_t = expert_ids.T
    (send,) = kernel_call(
        functools.partial(dispatch_body, cap, rows), [((rows, wide), BF16)],
        tokens, cotangent, ids_t, gates.T,
    )
    send, w1p, w2p = lax.optimization_barrier((send, w1p, w2p))
    own = lax.all_to_all(
        send.reshape(experts, cap, wide), "expert", split_axis=0, concat_axis=0, tiled=True
    ).reshape(rows, wide)

    chain_a, chain_b = [], []
    a, b = own, move(own, swap)
    for k in range(1, hops + 1):
        a = move(a, away)
        chain_a.append(a)
        if k < hops:
            b = move(b, away)
            chain_b.append(b)
    firsts = chain_a
    seconds = [own] + chain_b

    hid, pg, part = [], [], []
    ff = 2 * half
    for k in range(hops):
        h, p, r = kernel_call(
            work_body,
            [((2 * rows, ff), BF16), ((2 * rows, ff), BF16), ((2 * rows, slim), BF16)],
            firsts[k], seconds[k], w1, w1p, w2, w2p,
            flops=2 * 3 * 2 * rows * feat * ff,
        )
        hid.append(h)
        pg.append(p)
        part.append(r)

    s = move(part[hops - 1], home)
    for k in range(hops - 2, 0, -1):
        (s,) = kernel_call(functools.partial(plus_body, feat), [((2 * rows, slim), BF16)], s, part[k])
        s = move(s, home)
    sb = move(s[rows:], swap)
    (sa,) = kernel_call(functools.partial(plus_head_body, feat, rows), [((rows, slim), BF16)], s, part[0])
    sa = move(sa, home)
    (total,) = kernel_call(functools.partial(total_body, feat, rows), [((rows, slim), BF16)], sa, sb, part[0])
    back_rows = lax.all_to_all(
        total.reshape(experts, cap, slim), "expert", split_axis=0, concat_axis=0, tiled=True
    ).reshape(rows, slim)

    blocks = []
    for k in range(hops):
        blocks += [firsts[k], seconds[k]]
    x_all = jnp.concatenate([c[:, :feat] for c in blocks], axis=0)
    scaled_all = jnp.concatenate(
        [(c[:, 2 * feat : 2 * feat + 1].astype(F32) * c[:, feat : 2 * feat].astype(F32)).astype(BF16) for c in blocks],
        axis=0,
    )
    hidden_all = jnp.concatenate(hid, axis=0)
    pg_all = jnp.concatenate(pg, axis=0)
    grad_second = mm(hidden_all, scaled_all, ((0,), (0,)))
    grad_first = mm(x_all, pg_all, ((0,), (0,)))
    gs = move(grad_second[half:].astype(BF16), swap)
    gf = move(grad_first[:, half:].astype(BF16), swap)
    grad_out_weights = (grad_second[:half] + gs.astype(F32)).astype(BF16)[None]
    grad_in_weights = (grad_first[:, :half] + gf.astype(F32)).astype(BF16)[None]

    token_grads, gate_t = kernel_call(
        functools.partial(combine_body, cap, rows),
        [((tok, feat), BF16), ((2, tok), BF16)], back_rows, ids_t,
    )
    return (token_grads, gate_t.T, grad_in_weights, grad_out_weights)


def solution(mesh):
    in_specs = (
        P(("expert", "dp"), None),
        P(("expert", "dp"), None),
        P(("expert", "dp"), None),
        P(("expert", "dp"), None),
        P("expert", None, "dp"),
        P("expert", "dp", None),
    )
    out_specs = (
        P(("expert", "dp"), None),
        P(("expert", "dp"), None),
        P("expert", None, "dp"),
        P("expert", "dp", None),
    )

    return jax.shard_map(per_device, mesh=mesh, in_specs=in_specs, out_specs=out_specs, check_vma=False)
```

```python
import functools

import jax
import jax.numpy as jnp
from jax import lax
from jax.experimental import pallas as pl
from jax.experimental.pallas import tpu as pltpu
from jax.sharding import PartitionSpec as P


LANES = 128
F32, BF16 = jnp.float32, jnp.bfloat16


def mm(a, b, dims):
    return lax.dot_general(a, b, (dims, ((), ())), preferred_element_type=F32)


def kernel_call(body, out_shapes, *args, flops=0, limit=4):
    spec = pl.BlockSpec(memory_space=pltpu.VMEM)
    outs = tuple(jax.ShapeDtypeStruct(s, d) for s, d in out_shapes)
    moved = sum(a.size * a.dtype.itemsize for a in args)
    return pl.pallas_call(
        body,
        out_shape=outs,
        in_specs=[spec] * len(args),
        out_specs=tuple([spec] * len(outs)),
        compiler_params=pltpu.CompilerParams(vmem_limit_bytes=limit << 20),
        cost_estimate=pl.CostEstimate(flops=flops, bytes_accessed=moved, transcendentals=0),
    )(*args)


def matches(ids, cap, rows):
    tok = ids.shape[1]
    row = lax.broadcasted_iota(jnp.int32, (rows, tok), 0)
    expert, slot = row // cap, row % cap
    hit0 = (ids[0:1, :] == expert).astype(F32)
    hit1 = (ids[1:2, :] == expert).astype(F32)
    hit = hit0 + hit1
    earlier = (
        lax.broadcasted_iota(jnp.int32, (tok, tok), 0)
        < lax.broadcasted_iota(jnp.int32, (tok, tok), 1)
    ).astype(F32)
    before = mm(hit, earlier, ((1,), (0,)))
    held = hit * (before == slot.astype(F32)).astype(F32)
    return held, hit0, hit1


def dispatch_body(cap, rows, tok_hbm, cot_hbm, ids_hbm, gates_hbm, send_ref, tok_ref, cot_ref, ids_ref, gates_ref, sems):
    feat = tok_ref.shape[1]
    pairs = ((ids_hbm, ids_ref), (gates_hbm, gates_ref), (tok_hbm, tok_ref), (cot_hbm, cot_ref))
    copies = [pltpu.make_async_copy(a, b, sems.at[k]) for k, (a, b) in enumerate(pairs)]
    for c in copies:
        c.start()
    for c in copies:
        c.wait()
    held, hit0, hit1 = matches(ids_ref[...], cap, rows)
    gates = gates_ref[...].astype(F32)
    gate = jnp.sum(held * (hit0 * gates[0:1, :] + hit1 * gates[1:2, :]), axis=1, keepdims=True)
    pick = held.astype(BF16)
    send_ref[:, :feat] = mm(pick, tok_ref[...], ((1,), (0,))).astype(BF16)
    send_ref[:, feat:] = (gate * mm(pick, cot_ref[...], ((1,), (0,)))).astype(BF16)


def tail(gate_part):
    hi = gate_part.astype(BF16).astype(F32)
    lo = gate_part - hi
    lane = lax.broadcasted_iota(jnp.int32, (gate_part.shape[0], LANES), 1)
    return jnp.where(lane == 0, hi, jnp.where(lane == 1, lo, 0.0)).astype(BF16)


def work_body(a_ref, b_ref, w1_ref, w1p_ref, w2_ref, w2p_ref, hid_ref, pg_ref, pa_ref, pb_ref):
    feat = w1_ref.shape[0]
    half = w1_ref.shape[1]
    n = a_ref.shape[0]
    x = jnp.concatenate([a_ref[:, :feat], b_ref[:, :feat]], axis=0)
    scaled = jnp.concatenate([a_ref[:, feat:], b_ref[:, feat:]], axis=0)
    gate_part = jnp.zeros((2 * n, 1), F32)
    part = jnp.zeros((2 * n, feat), F32)
    for at, v1, v2 in ((0, w1_ref, w2_ref), (half, w1p_ref, w2p_ref)):
        pre = mm(x, v1[...], ((1,), (0,)))
        back = mm(scaled, v2[...], ((1,), (1,)))
        cdf = 0.5 * (1.0 + lax.erf(pre * 0.7071067811865476))
        pdf = 0.3989422804014327 * jnp.exp(-0.5 * pre * pre)
        hidden = (pre * cdf).astype(BF16)
        pre_grad = (back * (cdf + pre * pdf)).astype(BF16)
        hid_ref[:, at : at + half] = hidden
        pg_ref[:, at : at + half] = pre_grad
        gate_part += jnp.sum(hidden.astype(F32) * back, axis=1, keepdims=True)
        part += mm(pre_grad, v1[...], ((1,), (1,)))
    gates = tail(gate_part)
    pa_ref[:, :feat] = part[:n].astype(BF16)
    pb_ref[:, :feat] = part[n:].astype(BF16)
    pa_ref[:, feat:] = gates[:n]
    pb_ref[:, feat:] = gates[n:]


def plus_body(feat, *refs):
    *ins, out_ref = refs
    out_ref[:, :feat] = sum(r[:, :feat].astype(F32) for r in ins).astype(BF16)
    g = sum(r[:, feat:].astype(F32) for r in ins)
    out_ref[:, feat:] = tail(g[:, 0:1] + g[:, 1:2])


def combine_body(cap, rows, back_ref, ids_ref, gates_ref, tg_ref, gg_ref):
    feat = tg_ref.shape[1]
    held, hit0, hit1 = matches(ids_ref[...], cap, rows)
    tg_ref[...] = mm(held.astype(BF16), back_ref[:, :feat], ((0,), (0,))).astype(BF16)
    g = back_ref[:, feat:].astype(F32)
    g = g[:, 0:1] + g[:, 1:2]
    g0 = jnp.sum(held * hit0 * g, axis=0, keepdims=True)
    g1 = jnp.sum(held * hit1 * g, axis=0, keepdims=True)
    sums = jnp.concatenate([g0, g1], axis=0)
    gg_ref[...] = (sums / gates_ref[...].astype(F32)).astype(BF16)


def per_device(tokens, cotangent, expert_ids, gates, w_in, w_out):
    tok, feat = tokens.shape
    experts = lax.axis_size("expert")
    ndp = lax.axis_size("dp")
    nz = ndp // 2
    cap = max(2, 4 * tok // experts)
    rows = experts * cap
    hops = nz // 2
    wide = 2 * feat
    slim = feat + LANES

    swap = [(i, i ^ 1) for i in range(ndp)]

    def shifted(step, cross=0):
        pairs = []
        for z in range(nz):
            for core in range(2):
                up = step if core == 0 else -step
                pairs.append((2 * z + core, 2 * ((z + up) % nz) + (core ^ cross)))
        return pairs

    away, home = shifted(1), shifted(-1)
    over = shifted(-1, 1)

    def move(a, pairs):
        return lax.ppermute(a, "dp", pairs)

    w1 = w_in[0]
    w2 = w_out[0]
    half = w1.shape[1]
    w1p = move(w1, swap)
    w2p = move(w2, swap)

    ids_t, gates_t = expert_ids.T, gates.T
    taken = [pltpu.with_memory_space_constraint(a, pltpu.HBM) for a in (tokens, cotangent, ids_t, gates_t)]
    send = pl.pallas_call(
        functools.partial(dispatch_body, cap, rows),
        out_shape=jax.ShapeDtypeStruct((rows, wide), BF16),
        in_specs=[pl.BlockSpec(memory_space=pltpu.HBM)] * 4,
        out_specs=pl.BlockSpec(memory_space=pltpu.VMEM),
        scratch_shapes=[pltpu.VMEM(a.shape, a.dtype) for a in taken] + [pltpu.SemaphoreType.DMA((4,))],
        name="dispatch",
        compiler_params=pltpu.CompilerParams(vmem_limit_bytes=4 << 20),
    )(*taken)
    own = lax.all_to_all(
        send.reshape(experts, cap, wide), "expert", split_axis=0, concat_axis=0, tiled=True
    ).reshape(rows, wide)

    chain_a, chain_b = [], []
    a = b = own
    for k in range(1, hops + 1):
        a = move(a, away)
        chain_a.append(a)
        if k < hops:
            b = move(b, over if k == 1 else away)
            chain_b.append(b)
    firsts = chain_a
    seconds = chain_b + [own]

    hid, pg, part_a, part_b = [], [], [], []
    ff = 2 * half
    for k in range(hops):
        h, p, ra, rb = kernel_call(
            work_body,
            [((2 * rows, ff), BF16), ((2 * rows, ff), BF16), ((rows, slim), BF16), ((rows, slim), BF16)],
            firsts[k], seconds[k], w1, w1p, w2, w2p,
            limit=16, flops=2 * 3 * 2 * rows * feat * ff,
        )
        hid.append(h)
        pg.append(p)
        part_a.append(ra)
        part_b.append(rb)

    def plus(*args):
        return kernel_call(functools.partial(plus_body, feat), [((rows, slim), BF16)], *args)[0]

    sb = move(part_b[hops - 2], home)
    for k in range(hops - 3, -1, -1):
        sb = move(plus(sb, part_b[k]), over if k == 0 else home)
    sa = move(part_a[hops - 1], home)
    for k in range(hops - 2, -1, -1):
        sa = move(plus(sa, part_a[k]), home)
    total = plus(sa, sb, part_b[hops - 1])
    back_rows = lax.all_to_all(
        total.reshape(experts, cap, slim), "expert", split_axis=0, concat_axis=0, tiled=True
    ).reshape(rows, slim)

    blocks = []
    for k in range(hops):
        blocks += [firsts[k], seconds[k]]
    x_all = jnp.concatenate([c[:, :feat] for c in blocks], axis=0)
    scaled_all = jnp.concatenate([c[:, feat:] for c in blocks], axis=0)
    hidden_all = jnp.concatenate(hid, axis=0)
    pg_all = jnp.concatenate(pg, axis=0)
    peer_second = mm(hidden_all[:, half:], scaled_all, ((0,), (0,))).astype(BF16)
    peer_first = mm(x_all, pg_all[:, half:], ((0,), (0,))).astype(BF16)
    gs = move(peer_second, swap)
    gf = move(peer_first, swap)
    own_second = mm(hidden_all[:, :half], scaled_all, ((0,), (0,)))
    own_first = mm(x_all, pg_all[:, :half], ((0,), (0,)))
    grad_out_weights = (own_second + gs.astype(F32)).astype(BF16)[None]
    grad_in_weights = (own_first + gf.astype(F32)).astype(BF16)[None]

    token_grads, gate_t = kernel_call(
        functools.partial(combine_body, cap, rows),
        [((tok, feat), BF16), ((2, tok), BF16)], back_rows, ids_t, gates_t,
    )
    return (token_grads, gate_t.T, grad_in_weights, grad_out_weights)


def solution(mesh):
    in_specs = (
        P(("expert", "dp"), None),
        P(("expert", "dp"), None),
        P(("expert", "dp"), None),
        P(("expert", "dp"), None),
        P("expert", None, "dp"),
        P("expert", "dp", None),
    )
    out_specs = (
        P(("expert", "dp"), None),
        P(("expert", "dp"), None),
        P("expert", None, "dp"),
        P("expert", "dp", None),
    )

    return jax.shard_map(per_device, mesh=mesh, in_specs=in_specs, out_specs=out_specs, check_vma=False)
```

```python
import functools

import jax
import jax.numpy as jnp
from jax import lax
from jax.experimental import pallas as pl
from jax.experimental.pallas import tpu as pltpu
from jax.sharding import PartitionSpec as P


LANES = 128
F32, BF16 = jnp.float32, jnp.bfloat16


def mm(a, b, dims):
    return lax.dot_general(a, b, (dims, ((), ())), preferred_element_type=F32)


def kernel_call(body, out_shapes, *args, flops=0, limit=4):
    spec = pl.BlockSpec(memory_space=pltpu.VMEM)
    outs = tuple(jax.ShapeDtypeStruct(s, d) for s, d in out_shapes)
    moved = sum(a.size * a.dtype.itemsize for a in args)
    return pl.pallas_call(
        body,
        out_shape=outs,
        in_specs=[spec] * len(args),
        out_specs=tuple([spec] * len(outs)),
        compiler_params=pltpu.CompilerParams(vmem_limit_bytes=limit << 20),
        cost_estimate=pl.CostEstimate(flops=flops, bytes_accessed=moved, transcendentals=0),
    )(*args)


def matches(ids, cap, rows):
    tok = ids.shape[1]
    row = lax.broadcasted_iota(jnp.int32, (rows, tok), 0)
    expert, slot = row // cap, row % cap
    hit0 = (ids[0:1, :] == expert).astype(F32)
    hit1 = (ids[1:2, :] == expert).astype(F32)
    hit = hit0 + hit1
    earlier = (
        lax.broadcasted_iota(jnp.int32, (tok, tok), 0)
        < lax.broadcasted_iota(jnp.int32, (tok, tok), 1)
    ).astype(F32)
    before = mm(hit, earlier, ((1,), (0,)))
    held = hit * (before == slot.astype(F32)).astype(F32)
    return held, hit0, hit1


def dispatch_body(cap, rows, tok_hbm, cot_hbm, ids_hbm, gates_hbm, send_ref, tok_ref, cot_ref, ids_ref, gates_ref, sems):
    feat = tok_ref.shape[1]
    pairs = ((ids_hbm, ids_ref), (gates_hbm, gates_ref), (tok_hbm, tok_ref), (cot_hbm, cot_ref))
    copies = [pltpu.make_async_copy(a, b, sems.at[k]) for k, (a, b) in enumerate(pairs)]
    for c in copies:
        c.start()
    for c in copies:
        c.wait()
    held, hit0, hit1 = matches(ids_ref[...], cap, rows)
    gates = gates_ref[...].astype(F32)
    gate = jnp.sum(held * (hit0 * gates[0:1, :] + hit1 * gates[1:2, :]), axis=1, keepdims=True)
    pick = held.astype(BF16)
    send_ref[:, :feat] = mm(pick, tok_ref[...], ((1,), (0,))).astype(BF16)
    send_ref[:, feat:] = (gate * mm(pick, cot_ref[...], ((1,), (0,)))).astype(BF16)


def tail(gate_part):
    hi = gate_part.astype(BF16).astype(F32)
    lo = gate_part - hi
    lane = lax.broadcasted_iota(jnp.int32, (gate_part.shape[0], LANES), 1)
    return jnp.where(lane == 0, hi, jnp.where(lane == 1, lo, 0.0)).astype(BF16)


def work_body(count, *refs):
    blocks, (w1_ref, w1p_ref, w2_ref, w2p_ref) = refs[:count], refs[count : count + 4]
    hid_ref, pg_ref, *part_refs = refs[count + 4 :]
    feat, half = w1_ref.shape
    n = blocks[0].shape[0]
    x = jnp.concatenate([r[:, :feat] for r in blocks], axis=0)
    scaled = jnp.concatenate([r[:, feat:] for r in blocks], axis=0)
    gate_part = jnp.zeros((count * n, 1), F32)
    part = jnp.zeros((count * n, feat), F32)
    for at, v1, v2 in ((0, w1_ref, w2_ref), (half, w1p_ref, w2p_ref)):
        pre = mm(x, v1[...], ((1,), (0,)))
        back = mm(scaled, v2[...], ((1,), (1,)))
        cdf = 0.5 * (1.0 + lax.erf(pre * 0.7071067811865476))
        pdf = 0.3989422804014327 * jnp.exp(-0.5 * pre * pre)
        hidden = (pre * cdf).astype(BF16)
        pre_grad = (back * (cdf + pre * pdf)).astype(BF16)
        hid_ref[:, at : at + half] = hidden
        pg_ref[:, at : at + half] = pre_grad
        gate_part += jnp.sum(hidden.astype(F32) * back, axis=1, keepdims=True)
        part += mm(pre_grad, v1[...], ((1,), (1,)))
    gates = tail(gate_part)
    for k, part_ref in enumerate(part_refs):
        part_ref[:, :feat] = part[k * n : (k + 1) * n].astype(BF16)
        part_ref[:, feat:] = gates[k * n : (k + 1) * n]


def plus_body(feat, *refs):
    *ins, out_ref = refs
    out_ref[:, :feat] = sum(r[:, :feat].astype(F32) for r in ins).astype(BF16)
    g = sum(r[:, feat:].astype(F32) for r in ins)
    out_ref[:, feat:] = tail(g[:, 0:1] + g[:, 1:2])


def combine_body(cap, rows, back_ref, ids_ref, gates_ref, tg_ref, gg_ref):
    feat = tg_ref.shape[1]
    held, hit0, hit1 = matches(ids_ref[...], cap, rows)
    tg_ref[...] = mm(held.astype(BF16), back_ref[:, :feat], ((0,), (0,))).astype(BF16)
    g = back_ref[:, feat:].astype(F32)
    g = g[:, 0:1] + g[:, 1:2]
    g0 = jnp.sum(held * hit0 * g, axis=0, keepdims=True)
    g1 = jnp.sum(held * hit1 * g, axis=0, keepdims=True)
    sums = jnp.concatenate([g0, g1], axis=0)
    gg_ref[...] = (sums / gates_ref[...].astype(F32)).astype(BF16)


def per_device(tokens, cotangent, expert_ids, gates, w_in, w_out):
    tok, feat = tokens.shape
    experts = lax.axis_size("expert")
    ndp = lax.axis_size("dp")
    nz = ndp // 2
    cap = max(2, 4 * tok // experts)
    rows = experts * cap
    hops = nz // 2
    wide = 2 * feat
    slim = feat + LANES

    swap = [(i, i ^ 1) for i in range(ndp)]

    def shifted(step, cross):
        pairs = []
        for z in range(nz):
            for core in range(2):
                up = step if (z + core) % 2 == 0 else -step
                pairs.append((2 * z + core, 2 * ((z + up) % nz) + (core ^ cross)))
        return pairs

    away, home = shifted(1, 1), shifted(-1, 1)
    over = shifted(-1, 0)

    def move(a, pairs):
        return lax.ppermute(a, "dp", pairs)

    w1 = w_in[0]
    w2 = w_out[0]
    half = w1.shape[1]
    w1p = move(w1, swap)
    w2p = move(w2, swap)

    ids_t, gates_t = expert_ids.T, gates.T
    taken = [pltpu.with_memory_space_constraint(a, pltpu.HBM) for a in (tokens, cotangent, ids_t, gates_t)]
    send = pl.pallas_call(
        functools.partial(dispatch_body, cap, rows),
        out_shape=jax.ShapeDtypeStruct((rows, wide), BF16),
        in_specs=[pl.BlockSpec(memory_space=pltpu.HBM)] * 4,
        out_specs=pl.BlockSpec(memory_space=pltpu.VMEM),
        scratch_shapes=[pltpu.VMEM(a.shape, a.dtype) for a in taken] + [pltpu.SemaphoreType.DMA((4,))],
        name="dispatch",
        compiler_params=pltpu.CompilerParams(vmem_limit_bytes=4 << 20),
    )(*taken)
    own = lax.all_to_all(
        send.reshape(experts, cap, wide), "expert", split_axis=0, concat_axis=0, tiled=True
    ).reshape(rows, wide)

    chain_a, chain_b = [], []
    a = b = own
    for k in range(1, hops + 1):
        a = move(a, away)
        chain_a.append(a)
        if k < hops:
            b = move(b, over if k == 1 else away)
            chain_b.append(b)
    groups = [[chain_a[k], chain_b[k]] for k in range(hops - 1)] + [[chain_a[hops - 1], own]]

    hid, pg, part_a, part_b = [], [], [], []
    ff = 2 * half
    for group in groups:
        count = len(group)
        h, p, *parts = kernel_call(
            functools.partial(work_body, count),
            [((count * rows, ff), BF16)] * 2 + [((rows, slim), BF16)] * count,
            *group, w1, w1p, w2, w2p,
            limit=16, flops=2 * 3 * count * rows * feat * ff,
        )
        hid.append(h)
        pg.append(p)
        part_a.append(parts[0])
        part_b.append(parts[1])

    def plus(*args):
        return kernel_call(functools.partial(plus_body, feat), [((rows, slim), BF16)], *args)[0]

    sa = move(part_a[hops - 2], home)
    sb = move(part_b[hops - 2], home)
    join = 0
    jump = hops - 1 - join
    far = move(part_a[hops - 1], shifted(-jump, jump % 2))
    for k in range(hops - 3, -1, -1):
        sb = move(plus(sb, part_b[k]), over if k == 0 else home)
        extra = (far,) if k == join else ()
        sa = move(plus(sa, part_a[k], *extra), home)
    total = plus(sa, sb, part_b[hops - 1])
    back_rows = lax.all_to_all(
        total.reshape(experts, cap, slim), "expert", split_axis=0, concat_axis=0, tiled=True
    ).reshape(rows, slim)

    blocks = [c for group in groups for c in group]
    x_all = jnp.concatenate([c[:, :feat] for c in blocks], axis=0)
    scaled_all = jnp.concatenate([c[:, feat:] for c in blocks], axis=0)
    hidden_all = jnp.concatenate(hid, axis=0)
    pg_all = jnp.concatenate(pg, axis=0)
    peer_second = mm(hidden_all[:, half:], scaled_all, ((0,), (0,))).astype(BF16)
    peer_first = mm(x_all, pg_all[:, half:], ((0,), (0,))).astype(BF16)
    gs = move(peer_second, swap)
    gf = move(peer_first, swap)
    own_second = mm(hidden_all[:, :half], scaled_all, ((0,), (0,)))
    own_first = mm(x_all, pg_all[:, :half], ((0,), (0,)))
    grad_out_weights = (own_second + gs.astype(F32)).astype(BF16)[None]
    grad_in_weights = (own_first + gf.astype(F32)).astype(BF16)[None]

    token_grads, gate_t = kernel_call(
        functools.partial(combine_body, cap, rows),
        [((tok, feat), BF16), ((2, tok), BF16)], back_rows, ids_t, gates_t,
    )
    return (token_grads, gate_t.T, grad_in_weights, grad_out_weights)


def solution(mesh):
    in_specs = (
        P(("expert", "dp"), None),
        P(("expert", "dp"), None),
        P(("expert", "dp"), None),
        P(("expert", "dp"), None),
        P("expert", None, "dp"),
        P("expert", "dp", None),
    )
    out_specs = (
        P(("expert", "dp"), None),
        P(("expert", "dp"), None),
        P("expert", None, "dp"),
        P("expert", "dp", None),
    )

    return jax.shard_map(per_device, mesh=mesh, in_specs=in_specs, out_specs=out_specs, check_vma=False)
```

```python
import functools

import jax
import jax.numpy as jnp
from jax import lax
from jax.experimental import pallas as pl
from jax.experimental.pallas import tpu as pltpu
from jax.sharding import PartitionSpec as P


LANES = 128
F32, BF16 = jnp.float32, jnp.bfloat16


def mm(a, b, dims):
    return lax.dot_general(a, b, (dims, ((), ())), preferred_element_type=F32)


def kernel_call(body, out_shapes, *args, flops=0, limit=4):
    spec = pl.BlockSpec(memory_space=pltpu.VMEM)
    outs = tuple(jax.ShapeDtypeStruct(s, d) for s, d in out_shapes)
    moved = sum(a.size * a.dtype.itemsize for a in args)
    return pl.pallas_call(
        body,
        out_shape=outs,
        in_specs=[spec] * len(args),
        out_specs=tuple([spec] * len(outs)),
        compiler_params=pltpu.CompilerParams(vmem_limit_bytes=limit << 20),
        cost_estimate=pl.CostEstimate(flops=flops, bytes_accessed=moved, transcendentals=0),
    )(*args)


def matches(ids, cap, rows):
    tok = ids.shape[1]
    row = lax.broadcasted_iota(jnp.int32, (rows, tok), 0)
    expert, slot = row // cap, row % cap
    hit0 = (ids[0:1, :] == expert).astype(F32)
    hit1 = (ids[1:2, :] == expert).astype(F32)
    hit = hit0 + hit1
    earlier = (
        lax.broadcasted_iota(jnp.int32, (tok, tok), 0)
        < lax.broadcasted_iota(jnp.int32, (tok, tok), 1)
    ).astype(F32)
    before = mm(hit, earlier, ((1,), (0,)))
    held = hit * (before == slot.astype(F32)).astype(F32)
    return held, hit0, hit1


def dispatch_body(cap, rows, tok_hbm, cot_hbm, ids_hbm, gates_hbm, send_ref, tok_ref, cot_ref, ids_ref, gates_ref, sems):
    feat = tok_ref.shape[1]
    pairs = ((ids_hbm, ids_ref), (gates_hbm, gates_ref), (tok_hbm, tok_ref), (cot_hbm, cot_ref))
    copies = [pltpu.make_async_copy(a, b, sems.at[k]) for k, (a, b) in enumerate(pairs)]
    for c in copies:
        c.start()
    for c in copies:
        c.wait()
    held, hit0, hit1 = matches(ids_ref[...], cap, rows)
    gates = gates_ref[...].astype(F32)
    gate = jnp.sum(held * (hit0 * gates[0:1, :] + hit1 * gates[1:2, :]), axis=1, keepdims=True)
    pick = held.astype(BF16)
    send_ref[:, :feat] = mm(pick, tok_ref[...], ((1,), (0,))).astype(BF16)
    send_ref[:, feat:] = (gate * mm(pick, cot_ref[...], ((1,), (0,)))).astype(BF16)


def tail(gate_part):
    hi = gate_part.astype(BF16).astype(F32)
    lo = gate_part - hi
    lane = lax.broadcasted_iota(jnp.int32, (gate_part.shape[0], LANES), 1)
    return jnp.where(lane == 0, hi, jnp.where(lane == 1, lo, 0.0)).astype(BF16)


def work_body(count, *refs):
    blocks, (w1_ref, w1p_ref, w2_ref, w2p_ref) = refs[:count], refs[count : count + 4]
    hid_ref, pg_ref, *part_refs = refs[count + 4 :]
    feat, half = w1_ref.shape
    n = blocks[0].shape[0]
    x = jnp.concatenate([r[:, :feat] for r in blocks], axis=0)
    scaled = jnp.concatenate([r[:, feat:] for r in blocks], axis=0)
    gate_part = jnp.zeros((count * n, 1), F32)
    part = jnp.zeros((count * n, feat), F32)
    for at, v1, v2 in ((0, w1_ref, w2_ref), (half, w1p_ref, w2p_ref)):
        pre = mm(x, v1[...], ((1,), (0,)))
        back = mm(scaled, v2[...], ((1,), (1,)))
        cdf = 0.5 * (1.0 + lax.erf(pre * 0.7071067811865476))
        pdf = 0.3989422804014327 * jnp.exp(-0.5 * pre * pre)
        hidden = (pre * cdf).astype(BF16)
        pre_grad = (back * (cdf + pre * pdf)).astype(BF16)
        hid_ref[:, at : at + half] = hidden
        pg_ref[:, at : at + half] = pre_grad
        gate_part += jnp.sum(hidden.astype(F32) * back, axis=1, keepdims=True)
        part += mm(pre_grad, v1[...], ((1,), (1,)))
    gates = tail(gate_part)
    for k, part_ref in enumerate(part_refs):
        part_ref[:, :feat] = part[k * n : (k + 1) * n].astype(BF16)
        part_ref[:, feat:] = gates[k * n : (k + 1) * n]


def plus_body(feat, *refs):
    *ins, out_ref = refs
    out_ref[:, :feat] = sum(r[:, :feat].astype(F32) for r in ins).astype(BF16)
    g = sum(r[:, feat:].astype(F32) for r in ins)
    out_ref[:, feat:] = tail(g[:, 0:1] + g[:, 1:2])


def transposed_dot(parts, others):
    return mm(jnp.concatenate(parts, axis=0), jnp.concatenate(others, axis=0), ((0,), (0,)))


def grads_body(count, at, *refs):
    blocks, hid, pg = refs[: 2 * count], refs[2 * count : 3 * count], refs[3 * count : 4 * count]
    second_ref, first_ref = refs[4 * count :]
    feat, half = first_ref.shape
    second = transposed_dot([r[:, at : at + half] for r in hid], [r[:, feat:] for r in blocks])
    first = transposed_dot([r[:, :feat] for r in blocks], [r[:, at : at + half] for r in pg])
    second_ref[...] = second.astype(second_ref.dtype)
    first_ref[...] = first.astype(first_ref.dtype)


def combine_body(cap, rows, back_ref, ids_ref, gates_ref, tg_ref, gg_ref):
    feat = tg_ref.shape[1]
    held, hit0, hit1 = matches(ids_ref[...], cap, rows)
    tg_ref[...] = mm(held.astype(BF16), back_ref[:, :feat], ((0,), (0,))).astype(BF16)
    g = back_ref[:, feat:].astype(F32)
    g = g[:, 0:1] + g[:, 1:2]
    g0 = jnp.sum(held * hit0 * g, axis=0, keepdims=True)
    g1 = jnp.sum(held * hit1 * g, axis=0, keepdims=True)
    sums = jnp.concatenate([g0, g1], axis=0)
    gg_ref[...] = (sums / gates_ref[...].astype(F32)).astype(BF16)


def per_device(tokens, cotangent, expert_ids, gates, w_in, w_out):
    tok, feat = tokens.shape
    experts = lax.axis_size("expert")
    ndp = lax.axis_size("dp")
    nz = ndp // 2
    cap = max(2, 4 * tok // experts)
    rows = experts * cap
    hops = nz // 2
    wide = 2 * feat
    slim = feat + LANES

    swap = [(i, i ^ 1) for i in range(ndp)]

    def shifted(step, cross):
        pairs = []
        for z in range(nz):
            for core in range(2):
                up = step if (z + core) % 2 == 0 else -step
                pairs.append((2 * z + core, 2 * ((z + up) % nz) + (core ^ cross)))
        return pairs

    away, home = shifted(1, 1), shifted(-1, 1)
    over = shifted(-1, 0)

    def move(a, pairs):
        return lax.ppermute(a, "dp", pairs)

    w1 = w_in[0]
    w2 = w_out[0]
    half = w1.shape[1]
    w1p = move(w1, swap)
    w2p = move(w2, swap)

    ids_t, gates_t = expert_ids.T, gates.T
    taken = [pltpu.with_memory_space_constraint(a, pltpu.HBM) for a in (tokens, cotangent, ids_t, gates_t)]
    send = pl.pallas_call(
        functools.partial(dispatch_body, cap, rows),
        out_shape=jax.ShapeDtypeStruct((rows, wide), BF16),
        in_specs=[pl.BlockSpec(memory_space=pltpu.HBM)] * 4,
        out_specs=pl.BlockSpec(memory_space=pltpu.VMEM),
        scratch_shapes=[pltpu.VMEM(a.shape, a.dtype) for a in taken] + [pltpu.SemaphoreType.DMA((4,))],
        name="dispatch",
        compiler_params=pltpu.CompilerParams(vmem_limit_bytes=4 << 20),
    )(*taken)
    own = lax.all_to_all(
        send.reshape(experts, cap, wide), "expert", split_axis=0, concat_axis=0, tiled=True
    ).reshape(rows, wide)

    chain_a, chain_b = [], []
    a = b = own
    for k in range(1, hops + 1):
        a = move(a, away)
        chain_a.append(a)
        if k < hops:
            b = move(b, over if k == 1 else away)
            chain_b.append(b)
    groups = [[chain_a[k], chain_b[k]] for k in range(hops - 1)] + [[chain_a[hops - 1], own]]

    hid, pg, part_a, part_b = [], [], [], []
    ff = 2 * half
    for group in groups:
        count = len(group)
        h, p, *parts = kernel_call(
            functools.partial(work_body, count),
            [((count * rows, ff), BF16)] * 2 + [((rows, slim), BF16)] * count,
            *group, w1, w1p, w2, w2p,
            limit=16, flops=2 * 3 * count * rows * feat * ff,
        )
        hid.append(h)
        pg.append(p)
        part_a.append(parts[0])
        part_b.append(parts[1])

    def plus(*args):
        return kernel_call(functools.partial(plus_body, feat), [((rows, slim), BF16)], *args)[0]

    sa = move(part_a[hops - 2], home)
    sb = move(part_b[hops - 2], home)
    join = 0
    jump = hops - 1 - join
    far = move(part_a[hops - 1], shifted(-jump, jump % 2))
    for k in range(hops - 3, -1, -1):
        sb = move(plus(sb, part_b[k]), over if k == 0 else home)
        extra = (far,) if k == join else ()
        sa = move(plus(sa, part_a[k], *extra), home)
    total = plus(sa, sb, part_b[hops - 1])
    back_rows = lax.all_to_all(
        total.reshape(experts, cap, slim), "expert", split_axis=0, concat_axis=0, tiled=True
    ).reshape(rows, slim)

    blocks = [c for group in groups for c in group]
    held = blocks + hid + pg
    work = 4 * hops * 2 * rows * feat * half

    def grads(at, dtype):
        return kernel_call(
            functools.partial(grads_body, hops, at), [((half, feat), dtype), ((feat, half), dtype)],
            *held, limit=20, flops=work,
        )

    peer_second, peer_first = grads(half, BF16)
    gs = move(peer_second, swap)
    gf = move(peer_first, swap)
    x_all = jnp.concatenate([c[:, :feat] for c in blocks], axis=0)
    scaled_all = jnp.concatenate([c[:, feat:] for c in blocks], axis=0)
    hid_own = jnp.concatenate([h[:, :half] for h in hid], axis=0)
    pg_own = jnp.concatenate([p[:, :half] for p in pg], axis=0)
    own_second = mm(hid_own, scaled_all, ((0,), (0,)))
    own_first = mm(x_all, pg_own, ((0,), (0,)))
    grad_out_weights = (own_second + gs.astype(F32)).astype(BF16)[None]
    grad_in_weights = (own_first + gf.astype(F32)).astype(BF16)[None]

    token_grads, gate_t = kernel_call(
        functools.partial(combine_body, cap, rows),
        [((tok, feat), BF16), ((2, tok), BF16)], back_rows, ids_t, gates_t,
    )
    return (token_grads, gate_t.T, grad_in_weights, grad_out_weights)


def solution(mesh):
    in_specs = (
        P(("expert", "dp"), None),
        P(("expert", "dp"), None),
        P(("expert", "dp"), None),
        P(("expert", "dp"), None),
        P("expert", None, "dp"),
        P("expert", "dp", None),
    )
    out_specs = (
        P(("expert", "dp"), None),
        P(("expert", "dp"), None),
        P("expert", None, "dp"),
        P("expert", "dp", None),
    )

    return jax.shard_map(per_device, mesh=mesh, in_specs=in_specs, out_specs=out_specs, check_vma=False)
```

```python
import functools

import jax
import jax.numpy as jnp
from jax import lax
from jax.experimental import pallas as pl
from jax.experimental.pallas import tpu as pltpu
from jax.sharding import PartitionSpec as P


LANES = 128
F32, BF16 = jnp.float32, jnp.bfloat16


def mm(a, b, dims):
    return lax.dot_general(a, b, (dims, ((), ())), preferred_element_type=F32)


def kernel_call(body, out_shapes, *args, flops=0, limit=4):
    spec = pl.BlockSpec(memory_space=pltpu.VMEM)
    outs = tuple(jax.ShapeDtypeStruct(s, d) for s, d in out_shapes)
    moved = sum(a.size * a.dtype.itemsize for a in args)
    return pl.pallas_call(
        body,
        out_shape=outs,
        in_specs=[spec] * len(args),
        out_specs=tuple([spec] * len(outs)),
        compiler_params=pltpu.CompilerParams(vmem_limit_bytes=limit << 20),
        cost_estimate=pl.CostEstimate(flops=flops, bytes_accessed=moved, transcendentals=0),
    )(*args)


def matches(ids, cap, rows):
    tok = ids.shape[1]
    row = lax.broadcasted_iota(jnp.int32, (rows, tok), 0)
    expert, slot = row // cap, row % cap
    hit0 = (ids[0:1, :] == expert).astype(F32)
    hit1 = (ids[1:2, :] == expert).astype(F32)
    hit = hit0 + hit1
    earlier = (
        lax.broadcasted_iota(jnp.int32, (tok, tok), 0)
        < lax.broadcasted_iota(jnp.int32, (tok, tok), 1)
    ).astype(F32)
    before = mm(hit, earlier, ((1,), (0,)))
    held = hit * (before == slot.astype(F32)).astype(F32)
    return held, hit0, hit1


def dispatch_body(cap, rows, tok_hbm, cot_hbm, ids_hbm, gates_hbm, send_ref, tok_ref, cot_ref, ids_ref, gates_ref, sems):
    feat = tok_ref.shape[1]
    pairs = ((ids_hbm, ids_ref), (gates_hbm, gates_ref), (tok_hbm, tok_ref), (cot_hbm, cot_ref))
    copies = [pltpu.make_async_copy(a, b, sems.at[k]) for k, (a, b) in enumerate(pairs)]
    for c in copies:
        c.start()
    for c in copies:
        c.wait()
    held, hit0, hit1 = matches(ids_ref[...], cap, rows)
    gates = gates_ref[...].astype(F32)
    gate = jnp.sum(held * (hit0 * gates[0:1, :] + hit1 * gates[1:2, :]), axis=1, keepdims=True)
    pick = held.astype(BF16)
    send_ref[:, :feat] = mm(pick, tok_ref[...], ((1,), (0,))).astype(BF16)
    send_ref[:, feat:] = (gate * mm(pick, cot_ref[...], ((1,), (0,)))).astype(BF16)


def tail(gate_part):
    hi = gate_part.astype(BF16).astype(F32)
    lo = gate_part - hi
    lane = lax.broadcasted_iota(jnp.int32, (gate_part.shape[0], LANES), 1)
    return jnp.where(lane == 0, hi, jnp.where(lane == 1, lo, 0.0)).astype(BF16)


def work_body(count, *refs):
    blocks, (w1_ref, w1p_ref, w2_ref, w2p_ref) = refs[:count], refs[count : count + 4]
    hid_ref, pg_ref, *part_refs = refs[count + 4 :]
    feat, half = w1_ref.shape
    n = blocks[0].shape[0]
    x = jnp.concatenate([r[:, :feat] for r in blocks], axis=0)
    scaled = jnp.concatenate([r[:, feat:] for r in blocks], axis=0)
    gate_part = jnp.zeros((count * n, 1), F32)
    part = jnp.zeros((count * n, feat), F32)
    for at, v1, v2 in ((0, w1_ref, w2_ref), (half, w1p_ref, w2p_ref)):
        pre = mm(x, v1[...], ((1,), (0,)))
        back = mm(scaled, v2[...], ((1,), (1,)))
        cdf = 0.5 * (1.0 + lax.erf(pre * 0.7071067811865476))
        pdf = 0.3989422804014327 * jnp.exp(-0.5 * pre * pre)
        hidden = (pre * cdf).astype(BF16)
        pre_grad = (back * (cdf + pre * pdf)).astype(BF16)
        hid_ref[:, at : at + half] = hidden
        pg_ref[:, at : at + half] = pre_grad
        gate_part += jnp.sum(hidden.astype(F32) * back, axis=1, keepdims=True)
        part += mm(pre_grad, v1[...], ((1,), (1,)))
    gates = tail(gate_part)
    for k, part_ref in enumerate(part_refs):
        part_ref[:, :feat] = part[k * n : (k + 1) * n].astype(BF16)
        part_ref[:, feat:] = gates[k * n : (k + 1) * n]


def plus_body(feat, *refs):
    *ins, out_ref = refs
    out_ref[:, :feat] = sum(r[:, :feat].astype(F32) for r in ins).astype(BF16)
    g = sum(r[:, feat:].astype(F32) for r in ins)
    out_ref[:, feat:] = tail(g[:, 0:1] + g[:, 1:2])


def transposed_dot(parts, others):
    return mm(jnp.concatenate(parts, axis=0), jnp.concatenate(others, axis=0), ((0,), (0,)))


def grads_body(count, at, *refs):
    blocks, hid, pg = refs[: 2 * count], refs[2 * count : 3 * count], refs[3 * count : 4 * count]
    second_ref, first_ref = refs[4 * count :]
    feat, half = first_ref.shape
    second = transposed_dot([r[:, at : at + half] for r in hid], [r[:, feat:] for r in blocks])
    first = transposed_dot([r[:, :feat] for r in blocks], [r[:, at : at + half] for r in pg])
    second_ref[...] = second.astype(second_ref.dtype)
    first_ref[...] = first.astype(first_ref.dtype)


def total_body(feat, *refs):
    *ins, out_ref = refs
    shape = out_ref.shape[:2]
    out_ref[:, :, :feat] = sum(r[:, :feat].astype(F32) for r in ins).reshape(*shape, feat).astype(BF16)
    g = sum(r[:, feat:].astype(F32) for r in ins)
    lanes = tail(g[:, 0:1] + g[:, 1:2]).astype(F32)
    out_ref[:, :, feat:] = lanes.reshape(*shape, LANES).astype(BF16)


def combine_body(cap, rows, back_ref, ids_ref, gates_ref, tg_ref, gg_ref):
    feat = tg_ref.shape[1]
    held, hit0, hit1 = matches(ids_ref[...], cap, rows)
    tg_ref[...] = mm(held.astype(BF16), back_ref[:, :feat], ((0,), (0,))).astype(BF16)
    g = back_ref[:, feat:].astype(F32)
    g = g[:, 0:1] + g[:, 1:2]
    g0 = jnp.sum(held * hit0 * g, axis=0, keepdims=True)
    g1 = jnp.sum(held * hit1 * g, axis=0, keepdims=True)
    sums = jnp.concatenate([g0, g1], axis=0)
    gg_ref[...] = (sums / gates_ref[...].astype(F32)).astype(BF16)


def per_device(tokens, cotangent, expert_ids, gates, w_in, w_out):
    tok, feat = tokens.shape
    experts = lax.axis_size("expert")
    ndp = lax.axis_size("dp")
    nz = ndp // 2
    cap = max(2, 4 * tok // experts)
    rows = experts * cap
    hops = nz // 2
    wide = 2 * feat
    slim = feat + LANES

    swap = [(i, i ^ 1) for i in range(ndp)]

    def shifted(step, cross):
        pairs = []
        for z in range(nz):
            for core in range(2):
                up = step if (z + core) % 2 == 0 else -step
                pairs.append((2 * z + core, 2 * ((z + up) % nz) + (core ^ cross)))
        return pairs

    away, home = shifted(1, 1), shifted(-1, 1)
    over = shifted(-1, 0)

    def move(a, pairs):
        return lax.ppermute(a, "dp", pairs)

    w1 = w_in[0]
    w2 = w_out[0]
    half = w1.shape[1]
    w1p = move(w1, swap)
    w2p = move(w2, swap)

    ids_t, gates_t = expert_ids.T, gates.T
    taken = [pltpu.with_memory_space_constraint(a, pltpu.HBM) for a in (tokens, cotangent, ids_t, gates_t)]
    send = pl.pallas_call(
        functools.partial(dispatch_body, cap, rows),
        out_shape=jax.ShapeDtypeStruct((rows, wide), BF16),
        in_specs=[pl.BlockSpec(memory_space=pltpu.HBM)] * 4,
        out_specs=pl.BlockSpec(memory_space=pltpu.VMEM),
        scratch_shapes=[pltpu.VMEM(a.shape, a.dtype) for a in taken] + [pltpu.SemaphoreType.DMA((4,))],
        name="dispatch",
        compiler_params=pltpu.CompilerParams(vmem_limit_bytes=4 << 20),
    )(*taken)
    own = lax.all_to_all(
        send.reshape(experts, cap, wide), "expert", split_axis=0, concat_axis=0, tiled=True
    ).reshape(rows, wide)

    chain_a, chain_b = [], []
    a = b = own
    for k in range(1, hops + 1):
        a = move(a, away)
        chain_a.append(a)
        if k < hops:
            b = move(b, over if k == 1 else away)
            chain_b.append(b)
    groups = [[chain_a[k], chain_b[k]] for k in range(hops - 1)] + [[chain_a[hops - 1], own]]

    hid, pg, part_a, part_b = [], [], [], []
    ff = 2 * half
    for group in groups:
        count = len(group)
        h, p, *parts = kernel_call(
            functools.partial(work_body, count),
            [((count * rows, ff), BF16)] * 2 + [((rows, slim), BF16)] * count,
            *group, w1, w1p, w2, w2p,
            limit=16, flops=2 * 3 * count * rows * feat * ff,
        )
        hid.append(h)
        pg.append(p)
        part_a.append(parts[0])
        part_b.append(parts[1])

    def plus(*args):
        return kernel_call(functools.partial(plus_body, feat), [((rows, slim), BF16)], *args)[0]

    s = move(jnp.concatenate([part_a[hops - 2], part_b[hops - 2]], axis=0), home)
    sa, sb = s[:rows], s[rows:]
    join = 0
    jump = hops - 1 - join
    far = move(part_a[hops - 1], shifted(-jump, jump % 2))
    for k in range(hops - 3, -1, -1):
        sb = move(plus(sb, part_b[k]), over if k == 0 else home)
        extra = (far,) if k == join else ()
        sa = move(plus(sa, part_a[k], *extra), home)
    (total,) = kernel_call(
        functools.partial(total_body, feat), [((experts, cap, slim), BF16)],
        sa, sb, part_b[hops - 1],
    )
    back_rows = lax.all_to_all(total, "expert", split_axis=0, concat_axis=0, tiled=True).reshape(rows, slim)

    blocks = [c for group in groups for c in group]
    held = blocks + hid + pg
    work = 4 * hops * 2 * rows * feat * half

    def grads(at, dtype):
        return kernel_call(
            functools.partial(grads_body, hops, at), [((half, feat), dtype), ((feat, half), dtype)],
            *held, limit=20, flops=work,
        )

    peer_second, peer_first = grads(half, BF16)
    gs = move(peer_second, swap)
    gf = move(peer_first, swap)
    x_all = jnp.concatenate([c[:, :feat] for c in blocks], axis=0)
    scaled_all = jnp.concatenate([c[:, feat:] for c in blocks], axis=0)
    hid_own = jnp.concatenate([h[:, :half] for h in hid], axis=0)
    pg_own = jnp.concatenate([p[:, :half] for p in pg], axis=0)
    own_second = mm(hid_own, scaled_all, ((0,), (0,)))
    own_first = mm(x_all, pg_own, ((0,), (0,)))
    grad_out_weights = (own_second + gs.astype(F32)).astype(BF16)[None]
    grad_in_weights = (own_first + gf.astype(F32)).astype(BF16)[None]

    token_grads, gate_t = kernel_call(
        functools.partial(combine_body, cap, rows),
        [((tok, feat), BF16), ((2, tok), BF16)], back_rows, ids_t, gates_t,
    )
    return (token_grads, gate_t.T, grad_in_weights, grad_out_weights)


def solution(mesh):
    in_specs = (
        P(("expert", "dp"), None),
        P(("expert", "dp"), None),
        P(("expert", "dp"), None),
        P(("expert", "dp"), None),
        P("expert", None, "dp"),
        P("expert", "dp", None),
    )
    out_specs = (
        P(("expert", "dp"), None),
        P(("expert", "dp"), None),
        P("expert", None, "dp"),
        P("expert", "dp", None),
    )

    return jax.shard_map(per_device, mesh=mesh, in_specs=in_specs, out_specs=out_specs, check_vma=False)
```

```python
import functools

import jax
import jax.numpy as jnp
from jax import lax
from jax.experimental import pallas as pl
from jax.experimental.pallas import tpu as pltpu
from jax.sharding import PartitionSpec as P


LANES = 128
F32, BF16 = jnp.float32, jnp.bfloat16


def mm(a, b, dims):
    return lax.dot_general(a, b, (dims, ((), ())), preferred_element_type=F32)


def kernel_call(body, out_shapes, *args, flops=0, limit=4):
    spec = pl.BlockSpec(memory_space=pltpu.VMEM)
    outs = tuple(jax.ShapeDtypeStruct(s, d) for s, d in out_shapes)
    moved = sum(a.size * a.dtype.itemsize for a in args)
    return pl.pallas_call(
        body,
        out_shape=outs,
        in_specs=[spec] * len(args),
        out_specs=tuple([spec] * len(outs)),
        compiler_params=pltpu.CompilerParams(vmem_limit_bytes=limit << 20),
        cost_estimate=pl.CostEstimate(flops=flops, bytes_accessed=moved, transcendentals=0),
    )(*args)


def matches(ids, cap, rows):
    tok = ids.shape[1]
    row = lax.broadcasted_iota(jnp.int32, (rows, tok), 0)
    expert, slot = row // cap, row % cap
    hit0 = (ids[0:1, :] == expert).astype(F32)
    hit1 = (ids[1:2, :] == expert).astype(F32)
    hit = hit0 + hit1
    earlier = (
        lax.broadcasted_iota(jnp.int32, (tok, tok), 0)
        < lax.broadcasted_iota(jnp.int32, (tok, tok), 1)
    ).astype(F32)
    before = mm(hit, earlier, ((1,), (0,)))
    held = hit * (before == slot.astype(F32)).astype(F32)
    return held, hit0, hit1


def dispatch_body(cap, rows, tok_hbm, cot_hbm, ids_hbm, gates_hbm, send_ref, tok_ref, cot_ref, ids_ref, gates_ref, sems):
    feat = tok_ref.shape[1]
    pairs = ((ids_hbm, ids_ref), (gates_hbm, gates_ref), (tok_hbm, tok_ref), (cot_hbm, cot_ref))
    copies = [pltpu.make_async_copy(a, b, sems.at[k]) for k, (a, b) in enumerate(pairs)]
    for c in copies:
        c.start()
    for c in copies:
        c.wait()
    held, hit0, hit1 = matches(ids_ref[...], cap, rows)
    gates = gates_ref[...].astype(F32)
    gate = jnp.sum(held * (hit0 * gates[0:1, :] + hit1 * gates[1:2, :]), axis=1, keepdims=True)
    pick = held.astype(BF16)
    send_ref[:, :feat] = mm(pick, tok_ref[...], ((1,), (0,))).astype(BF16)
    send_ref[:, feat:] = (gate * mm(pick, cot_ref[...], ((1,), (0,)))).astype(BF16)


def tail(gate_part):
    hi = gate_part.astype(BF16).astype(F32)
    lo = gate_part - hi
    lane = lax.broadcasted_iota(jnp.int32, (gate_part.shape[0], LANES), 1)
    return jnp.where(lane == 0, hi, jnp.where(lane == 1, lo, 0.0)).astype(BF16)


def work_body(count, *refs):
    blocks, (w1_ref, w1p_ref, w2_ref, w2p_ref) = refs[:count], refs[count : count + 4]
    hid_ref, pg_ref, *part_refs = refs[count + 4 :]
    feat, half = w1_ref.shape
    n = blocks[0].shape[0]
    x = jnp.concatenate([r[:, :feat] for r in blocks], axis=0)
    scaled = jnp.concatenate([r[:, feat:] for r in blocks], axis=0)
    gate_part = jnp.zeros((count * n, 1), F32)
    part = jnp.zeros((count * n, feat), F32)
    for at, v1, v2 in ((0, w1_ref, w2_ref), (half, w1p_ref, w2p_ref)):
        pre = mm(x, v1[...], ((1,), (0,)))
        back = mm(scaled, v2[...], ((1,), (1,)))
        cdf = 0.5 * (1.0 + lax.erf(pre * 0.7071067811865476))
        pdf = 0.3989422804014327 * jnp.exp(-0.5 * pre * pre)
        hidden = (pre * cdf).astype(BF16)
        pre_grad = (back * (cdf + pre * pdf)).astype(BF16)
        hid_ref[:, at : at + half] = hidden
        pg_ref[:, at : at + half] = pre_grad
        gate_part += jnp.sum(hidden.astype(F32) * back, axis=1, keepdims=True)
        part += mm(pre_grad, v1[...], ((1,), (1,)))
    gates = tail(gate_part)
    for k, part_ref in enumerate(part_refs):
        part_ref[:, :feat] = part[k * n : (k + 1) * n].astype(BF16)
        part_ref[:, feat:] = gates[k * n : (k + 1) * n]


def plus_body(feat, *refs):
    *ins, out_ref = refs
    out_ref[:, :feat] = sum(r[:, :feat].astype(F32) for r in ins).astype(BF16)
    g = sum(r[:, feat:].astype(F32) for r in ins)
    out_ref[:, feat:] = tail(g[:, 0:1] + g[:, 1:2])


def transposed_dot(parts, others):
    return mm(jnp.concatenate(parts, axis=0), jnp.concatenate(others, axis=0), ((0,), (0,)))


def grads_body(count, at, *refs):
    blocks, hid, pg = refs[: 2 * count], refs[2 * count : 3 * count], refs[3 * count : 4 * count]
    second_ref, first_ref = refs[4 * count :]
    feat, half = first_ref.shape
    second = transposed_dot([r[:, at : at + half] for r in hid], [r[:, feat:] for r in blocks])
    first = transposed_dot([r[:, :feat] for r in blocks], [r[:, at : at + half] for r in pg])
    second_ref[...] = second.astype(second_ref.dtype)
    first_ref[...] = first.astype(first_ref.dtype)


def total_body(feat, *refs):
    *ins, out_ref = refs
    shape = out_ref.shape[:2]
    out_ref[:, :, :feat] = sum(r[:, :feat].astype(F32) for r in ins).reshape(*shape, feat).astype(BF16)
    g = sum(r[:, feat:].astype(F32) for r in ins)
    lanes = tail(g[:, 0:1] + g[:, 1:2]).astype(F32)
    out_ref[:, :, feat:] = lanes.reshape(*shape, LANES).astype(BF16)


def combine_body(cap, rows, back_ref, ids_ref, gates_ref, tg_ref, gg_ref):
    feat = tg_ref.shape[1]
    held, hit0, hit1 = matches(ids_ref[...], cap, rows)
    back = back_ref[...].astype(F32).reshape(rows, back_ref.shape[2])
    tg_ref[...] = mm(held.astype(BF16), back[:, :feat].astype(BF16), ((0,), (0,))).astype(BF16)
    g = back[:, feat:]
    g = g[:, 0:1] + g[:, 1:2]
    g0 = jnp.sum(held * hit0 * g, axis=0, keepdims=True)
    g1 = jnp.sum(held * hit1 * g, axis=0, keepdims=True)
    sums = jnp.concatenate([g0, g1], axis=0)
    gg_ref[...] = (sums / gates_ref[...].astype(F32)).astype(BF16)


def per_device(tokens, cotangent, expert_ids, gates, w_in, w_out):
    tok, feat = tokens.shape
    experts = lax.axis_size("expert")
    ndp = lax.axis_size("dp")
    nz = ndp // 2
    cap = max(2, 4 * tok // experts)
    rows = experts * cap
    hops = nz // 2
    wide = 2 * feat
    slim = feat + LANES

    swap = [(i, i ^ 1) for i in range(ndp)]

    def shifted(step, cross):
        pairs = []
        for z in range(nz):
            for core in range(2):
                up = step if (z + core) % 2 == 0 else -step
                pairs.append((2 * z + core, 2 * ((z + up) % nz) + (core ^ cross)))
        return pairs

    away, home = shifted(1, 1), shifted(-1, 1)
    over = shifted(-1, 0)

    def move(a, pairs):
        return lax.ppermute(a, "dp", pairs)

    w1 = w_in[0]
    w2 = w_out[0]
    half = w1.shape[1]
    w1p = move(w1, swap)
    w2p = move(w2, swap)

    ids_t, gates_t = expert_ids.T, gates.T
    taken = [pltpu.with_memory_space_constraint(a, pltpu.HBM) for a in (tokens, cotangent, ids_t, gates_t)]
    send = pl.pallas_call(
        functools.partial(dispatch_body, cap, rows),
        out_shape=jax.ShapeDtypeStruct((rows, wide), BF16),
        in_specs=[pl.BlockSpec(memory_space=pltpu.HBM)] * 4,
        out_specs=pl.BlockSpec(memory_space=pltpu.VMEM),
        scratch_shapes=[pltpu.VMEM(a.shape, a.dtype) for a in taken] + [pltpu.SemaphoreType.DMA((4,))],
        name="dispatch",
        compiler_params=pltpu.CompilerParams(vmem_limit_bytes=4 << 20),
    )(*taken)
    own = lax.all_to_all(
        send.reshape(experts, cap, wide), "expert", split_axis=0, concat_axis=0, tiled=True
    ).reshape(rows, wide)

    chain_a, chain_b = [], []
    a = b = own
    for k in range(1, hops + 1):
        a = move(a, away)
        chain_a.append(a)
        if k < hops:
            b = move(b, over if k == 1 else away)
            chain_b.append(b)
    groups = [[chain_a[k], chain_b[k]] for k in range(hops - 1)] + [[chain_a[hops - 1], own]]

    hid, pg, part_a, part_b = [], [], [], []
    ff = 2 * half
    for group in groups:
        count = len(group)
        h, p, *parts = kernel_call(
            functools.partial(work_body, count),
            [((count * rows, ff), BF16)] * 2 + [((rows, slim), BF16)] * count,
            *group, w1, w1p, w2, w2p,
            limit=16, flops=2 * 3 * count * rows * feat * ff,
        )
        hid.append(h)
        pg.append(p)
        part_a.append(parts[0])
        part_b.append(parts[1])

    def plus(*args):
        return kernel_call(functools.partial(plus_body, feat), [((rows, slim), BF16)], *args)[0]

    s = move(jnp.concatenate([part_a[hops - 2], part_b[hops - 2]], axis=0), home)
    sa, sb = s[:rows], s[rows:]
    join = 0
    jump = hops - 1 - join
    far = move(part_a[hops - 1], shifted(-jump, jump % 2))
    for k in range(hops - 3, -1, -1):
        sb = move(plus(sb, part_b[k]), over if k == 0 else home)
        extra = (far,) if k == join else ()
        sa = move(plus(sa, part_a[k], *extra), home)
    (total,) = kernel_call(
        functools.partial(total_body, feat), [((experts, cap, slim), BF16)],
        sa, sb, part_b[hops - 1],
    )
    back_rows = lax.all_to_all(total, "expert", split_axis=0, concat_axis=0, tiled=True)

    blocks = [c for group in groups for c in group]
    held = blocks + hid + pg
    work = 4 * hops * 2 * rows * feat * half

    def grads(at, dtype):
        return kernel_call(
            functools.partial(grads_body, hops, at), [((half, feat), dtype), ((feat, half), dtype)],
            *held, limit=20, flops=work,
        )

    peer_second, peer_first = grads(half, BF16)
    gs = move(peer_second, swap)
    gf = move(peer_first, swap)
    x_all = jnp.concatenate([c[:, :feat] for c in blocks], axis=0)
    scaled_all = jnp.concatenate([c[:, feat:] for c in blocks], axis=0)
    hid_own = jnp.concatenate([h[:, :half] for h in hid], axis=0)
    pg_own = jnp.concatenate([p[:, :half] for p in pg], axis=0)
    own_second = mm(hid_own, scaled_all, ((0,), (0,)))
    own_first = mm(x_all, pg_own, ((0,), (0,)))
    grad_out_weights = (own_second + gs.astype(F32)).astype(BF16)[None]
    grad_in_weights = (own_first + gf.astype(F32)).astype(BF16)[None]

    token_grads, gate_t = kernel_call(
        functools.partial(combine_body, cap, rows),
        [((tok, feat), BF16), ((2, tok), BF16)], back_rows, ids_t, gates_t,
    )
    return (token_grads, gate_t.T, grad_in_weights, grad_out_weights)


def solution(mesh):
    in_specs = (
        P(("expert", "dp"), None),
        P(("expert", "dp"), None),
        P(("expert", "dp"), None),
        P(("expert", "dp"), None),
        P("expert", None, "dp"),
        P("expert", "dp", None),
    )
    out_specs = (
        P(("expert", "dp"), None),
        P(("expert", "dp"), None),
        P("expert", None, "dp"),
        P("expert", "dp", None),
    )

    return jax.shard_map(per_device, mesh=mesh, in_specs=in_specs, out_specs=out_specs, check_vma=False)
```
